128 devices in a mesh: row: 8 (over x_hi, y), col: 16 (over x_lo, z, core).
Axes of the slice: x: 4 (x_hi: 2, x_lo: 2; x = x_hi * 2 + x_lo), y: 4, z: 4, core: 2. Of those that a mesh axis runs over, the one named last changes fastest.
Arguments:
- matrix: float32 [32768, 8192], P('row', 'col'), may hold values from -6 to 6
- pivots: int32 [1024], replicated, may hold values from 0 to 32767, as said below
- lower_panel: float32 [1024, 32768], P('col', 'row'), as said below
Outputs:
- updated: float32 [32768, 8192], P('row', 'col')
The draws below stay inside these ranges and needn't reach their ends.
Inputs may be any that keep to these rules, and one draw needn't show every extreme that they name: `pivots`: the 1024 entries are distinct rows of the trailing matrix. For column index r < 1024: lower_panel[r, r] = 1 and lower_panel[k, r] = 0 for k > r.
All inputs are finite; a program needn't handle non-finite values.
Results may differ from the reference program's by a relative error of at most 0.000059.
Values sent between devices are 32-bit elements; how exact they have to be, the bound alone decides.
No kernel may reach another device: no remote copies, remote signals or barrier semaphores. Data moves between devices by JAX's collectives and lax.ppermute only.
A program may use at most 128 MiB of HBM per device.

```python
import math
import jax
import jax.numpy as jnp
from jax import lax

NB = 1024
R_DEV = 4096
M = 32768
N = 8192
N_ROW = 8


def shuffle_rows(subkey):
    return jax.random.permutation(subkey, R_DEV).astype(jnp.int32)


def draw_pivots(key, part):
    first_key, second_key, third_key = jax.random.split(key, 3)
    owner = jnp.minimum(jax.random.randint(first_key, (NB,), 0, N_ROW), jax.random.randint(second_key, (NB,), 0, N_ROW)).astype(jnp.int32)
    one_hot = (owner[:, None] == jnp.arange(N_ROW, dtype=jnp.int32)[None, :]).astype(jnp.int32)
    ranking = jnp.sum((jnp.cumsum(one_hot, axis=0) - one_hot) * one_hot, axis=1)
    orders = jax.vmap(shuffle_rows)(jax.random.split(third_key, N_ROW))
    return (owner * R_DEV + orders[owner, ranking]).astype(jnp.int32)


def draw_lower_panel(key, part):
    first_key = jax.random.fold_in(key, 0)
    values = jax.random.normal(first_key, (NB, M), jnp.float32) * (1.0 / math.sqrt(NB))
    krow = jnp.arange(NB, dtype=jnp.int32)[:, None]
    rcol = jnp.arange(M, dtype=jnp.int32)[None, :]
    upper = jnp.where(krow < rcol, values, jnp.where(krow == rcol, 1.0, 0.0))
    return jnp.where(rcol < NB, upper, values).astype(jnp.float32)


def block_scale(own_key, shape, cuts, least, top_value):
    def one(dim, parts):
        draws = jax.random.uniform(jax.random.fold_in(jax.random.fold_in(own_key, 6), dim), (parts,), jnp.float32, least / len(cuts), top_value / len(cuts))
        return jnp.repeat(jnp.exp(draws), shape[dim] // parts).reshape((-1,) + (1,) * (len(shape) - dim - 1))

    gain = one(*cuts[0])
    for cut in cuts[1:]:
        gain = gain * one(*cut)
    return gain


def bell_draw(own_key, dims, deviation, bound, pieces=(), held_as=jnp.bfloat16):
    drawn = deviation * jax.random.normal(own_key, dims, jnp.float32)
    if pieces:
        drawn = drawn * block_scale(own_key, dims, pieces, -0.22, 0.18)
    return jnp.clip(drawn, -bound, bound).astype(held_as)


def setup_inputs(seed: int = 0) -> dict:
    splits = jax.random.split(jax.random.key(seed), 4)
    return {
        "matrix": bell_draw(splits[0], (M, N), 1.0, 6.0, ((0, 8), (1, 16)), jnp.float32),
        "pivots": draw_pivots(jax.random.fold_in(splits[3], 71), 0),
        "lower_panel": draw_lower_panel(jax.random.fold_in(splits[3], 71), 0),
    }


def displaced_rows(pivots, top):
    whole = jnp.arange(top, dtype=jnp.int32)
    chosen_top = jnp.any(pivots[None, :] == whole[:, None], axis=1)
    spare_rows = jnp.sort(jnp.where(chosen_top, jnp.int32(2 ** 30), whole))
    vacated = jnp.sort(jnp.where(pivots >= top, pivots, jnp.int32(2 ** 30)))
    return spare_rows, vacated


def reference(matrix, pivots, lower_panel):
    top = pivots.shape[0]
    total_rows = matrix.shape[0]
    spare_rows, vacated = displaced_rows(pivots, top)
    pivot_block = matrix[pivots]
    target = jnp.where(vacated < 2 ** 30, vacated, total_rows).astype(jnp.int32)
    source = matrix[jnp.minimum(spare_rows, top - 1)]
    swapped = matrix.at[target].set(source, mode="drop")
    product = jnp.dot(lower_panel.T, pivot_block, precision=lax.Precision.HIGHEST, preferred_element_type=jnp.float32)
    row_index = jnp.arange(total_rows, dtype=jnp.int32)[:, None]
    return jnp.where(row_index < top, product, swapped - product)
```

```python
import functools

import jax
import jax.numpy as jnp
from jax import lax
from jax.experimental import pallas as pl
from jax.experimental.pallas import tpu as pltpu
from jax.sharding import PartitionSpec as P


NZ, NY, NX, NC = 4, 4, 2, 2


def col_shift(dx, dz, dc):
    pairs = []
    for i in range(NX * NZ * NC):
        x, z, c = i // 8, (i // 2) % 4, i % 2
        pairs.append((i, ((x + dx) % 2) * 8 + ((z + dz) % 4) * 2 + (c + dc) % 2))
    return pairs


def row_shift(dx, dy, keep=lambda x: True):
    pairs = []
    for i in range(NX * NY):
        x, y = i // 4, i % 4
        if keep(x):
            pairs.append((i, ((x + dx) % 2) * 4 + (y + dy) % 4))
    return pairs


def send_col(value, dx, dz, dc=0):
    return lax.ppermute(value, "col", col_shift(dx, dz, dc))


def send_row(value, dx, dy):
    return lax.ppermute(value, "row", row_shift(dx, dy))


FIRST = [(0, 0), (1, 0), (0, -1), (0, 1), (0, 2)]
SECOND = [(1, -1), (1, 1), (1, 2)]
KP = 64


def split(value):
    hi = value.astype(jnp.bfloat16)
    return hi, (value - hi.astype(jnp.float32)).astype(jnp.bfloat16)


def prep_body(order_ref, *refs):
    slices, (b1h, b1l, b2h, b2l), full = refs[:4], refs[4:8], refs[8]
    y = order_ref[16]
    for d in range(4):
        t = lax.rem(y + d, 4)
        full[pl.ds(pl.multiple_of(t * 256, 256), 256), :] = slices[d][...]
    n1 = 2 * len(FIRST)
    for j in range(16):
        rows = full[pl.ds(pl.multiple_of(order_ref[j] * KP, KP), KP), :]
        hi, lo = split(rows)
        if j < n1:
            b1h[j * KP : (j + 1) * KP, :] = hi
            b1l[j * KP : (j + 1) * KP, :] = lo
        else:
            k = j - n1
            b2h[k * KP : (k + 1) * KP, :] = hi
            b2l[k * KP : (k + 1) * KP, :] = lo


def prep(order, slices):
    n = slices[0].shape[1]
    k1, k2 = 2 * len(FIRST) * KP, 2 * len(SECOND) * KP
    out = [jax.ShapeDtypeStruct((k, n), jnp.bfloat16) for k in (k1, k1, k2, k2)]
    vm = pl.BlockSpec(memory_space=pltpu.VMEM)
    return pl.pallas_call(
        prep_body,
        in_specs=[pl.BlockSpec(memory_space=pltpu.SMEM)] + [vm] * 4,
        out_specs=[vm] * 4,
        out_shape=out,
        scratch_shapes=[pltpu.VMEM((1024, n), jnp.float32)],
        cost_estimate=pl.CostEstimate(flops=0, bytes_accessed=4 << 20, transcendentals=0),
        name="prep",
    )(order, *slices)


def product(pieces, bh, bl, ah, al):
    for j, piece in enumerate(pieces):
        hi, lo = split(piece[...])
        ah[j * KP : (j + 1) * KP, :] = hi
        al[j * KP : (j + 1) * KP, :] = lo
    dot = functools.partial(
        lax.dot_general,
        dimension_numbers=(((0,), (0,)), ((), ())),
        preferred_element_type=jnp.float32,
    )
    return dot(ah[...], bh[...]) + dot(ah[...], bl[...]) + dot(al[...], bh[...])


MB = 512


def first_body(block0, npc, info, starts, keys, spares, *refs):
    pieces = refs[:npc]
    bh, bl, mat, top = refs[npc : npc + 4]
    out, ah, al = refs[-3:]
    block = pl.program_id(0) + block0
    root = info[0]
    in_top = (root == 1) & (block < 1024 // MB)
    out[...] = jnp.where(in_top, 0.0, mat[...])

    def patch(k, carry):
        r = keys[k] - block * MB

        @pl.when(root == 1)
        def _():
            out[pl.ds(r, 1), :] = top[pl.ds(spares[k], 1), :]

        @pl.when(root == 0)
        def _():
            out[pl.ds(r, 1), :] = jnp.zeros((1, out.shape[1]), jnp.float32)

        return carry

    lax.fori_loop(starts[block], starts[block + 1], patch, 0)
    sign = jnp.where(in_top, 1.0, -1.0)
    out[...] += sign * product(pieces, bh, bl, ah, al)


def second_body(block0, npc, info, starts, keys, slots, *refs):
    pieces = refs[:npc]
    bh, bl, prev, disp = refs[npc : npc + 4]
    out, ah, al = refs[-3:]
    block = pl.program_id(0) + block0
    root = info[0]
    in_top = (root == 1) & (block < 1024 // MB)
    sign = jnp.where(in_top, 1.0, -1.0)
    out[...] = prev[...] + sign * product(pieces, bh, bl, ah, al)

    def patch(k, carry):
        r = keys[k] - block * MB
        out[pl.ds(r, 1), :] += disp[pl.ds(slots[k], 1), :]
        return carry

    @pl.when(root == 0)
    def _():
        lax.fori_loop(starts[block], starts[block + 1], patch, 0)


def update(body, name, half, scalars, pieces, whole, bh, bl, base, rows, prev):
    n = base.shape[1]
    nblk = 2048 // MB
    block0 = half * nblk
    npc = len(pieces)
    specs = [
        pl.BlockSpec((KP, MB), (lambda i, *_: (0, i + block0)) if w else (lambda i, *_: (0, i)))
        for w in whole
    ]
    const = functools.partial(pl.BlockSpec, index_map=lambda i, *_: (0, 0), pipeline_mode=pl.Buffered(1))
    specs += [const(bh.shape), const(bl.shape)]
    specs += [pl.BlockSpec((MB, n), lambda i, *_: (i + block0, 0)), const((1024, n))]
    args = [*pieces, bh, bl, base, rows]
    aliases = {}
    if prev is not None:
        if prev is base:
            aliases = {4 + npc + 2: 0}
        else:
            specs.append(pl.BlockSpec(memory_space=pl.ANY))
            args.append(prev)
            aliases = {4 + npc + 4: 0}
    k = npc * KP
    return pl.pallas_call(
        functools.partial(body, block0, npc),
        grid_spec=pltpu.PrefetchScalarGridSpec(
            num_scalar_prefetch=4,
            grid=(nblk,),
            in_specs=specs,
            out_specs=pl.BlockSpec((MB, n), lambda i, *_: (i + block0, 0)),
            scratch_shapes=[pltpu.VMEM((k, MB), jnp.bfloat16)] * 2,
        ),
        out_shape=jax.ShapeDtypeStruct(base.shape, jnp.float32),
        input_output_aliases=aliases,
        cost_estimate=pl.CostEstimate(
            flops=6 * 2048 * n * k, bytes_accessed=4 * (2048 * k + 4096 * n + k * n), transcendentals=0
        ),
        name=name,
    )(*scalars, *args)


def per_device(matrix, pivots, lower_panel):
    top = pivots.shape[0]
    local_rows, n = matrix.shape
    row, col = lax.axis_index("row"), lax.axis_index("col")
    x_hi, y = row // 4, row % 4
    x_lo, z, core = col // 8, (col // 2) % 4, col % 2
    first_row = row * local_rows
    root = row == 0

    half = local_rows // 2
    own = [lower_panel[:, :half], lower_panel[:, half:]]
    zm = [send_col(o, 0, 1) for o in own]
    zp = [send_col(o, 0, -1) for o in own]
    xs = [send_col(o, 1, 0) for o in own]
    own_other = send_col(lower_panel, 0, 0, 1)

    tops = jnp.arange(top, dtype=jnp.int32)
    chosen = jnp.any(pivots[None, :] == tops[:, None], axis=1)
    away = pivots >= top
    rank = jnp.sum((away & (pivots[None, :] < pivots[:, None])).astype(jnp.int32), axis=1)
    before = jnp.sum((~chosen[None, :] & (tops[None, :] < tops[:, None])).astype(jnp.int32), axis=1)
    hit = ~chosen[None, :] & (before[None, :] == rank[:, None])
    spare = jnp.sum(jnp.where(hit, tops[None, :], 0), axis=1)
    owned = (pivots >= first_row) & (pivots < first_row + local_rows)
    index = jnp.where(owned, pivots - first_row, jnp.where(root, spare, 0))
    live = owned | root

    quarter = top // 4

    def gathered(d):
        start = ((y + d) % 4) * quarter
        idx = lax.dynamic_slice(index, (start,), (quarter,))
        msk = lax.dynamic_slice(live, (start,), (quarter,))
        return jnp.where(msk[:, None], jnp.take(matrix, idx, axis=0, mode="clip"), 0.0)

    g2 = gathered(2)
    m2 = send_row(g2, 0, 2)
    g1 = gathered(1)
    m1 = send_row(g1, 0, 1)
    g3 = gathered(3)
    m3 = send_row(g3, 0, -1)
    g0 = gathered(0)
    root_owned = lax.dynamic_slice(pivots, (y * quarter,), (quarter,)) < local_rows
    pivot_sum, disp = 0.0, 0.0
    for message, source in ((g0, y), (m1, (y + 3) % 4), (m2, (y + 2) % 4), (m3, (y + 1) % 4)):
        from_root = (x_hi == 0) & (source == 0)
        is_disp = from_root & ~root_owned[:, None]
        pivot_sum = pivot_sum + jnp.where(is_disp, 0.0, message)
        disp = disp + jnp.where(is_disp, message, 0.0)
    pivot_part = pivot_sum + send_row(pivot_sum, 1, 0)
    cross = lax.ppermute(disp, "row", row_shift(1, 0, lambda x: x == 0))
    disp = jnp.where(x_hi == 0, disp, cross)

    def gather_y(part):
        lo = send_row(part, 0, 1)
        hi = send_row(part, 0, -1)
        far_l = send_row(lo[:, : n // 2], 0, 1)
        far_r = send_row(hi[:, n // 2 :], 0, -1)
        return [part, hi, jnp.concatenate([far_l, far_r], axis=1), lo]

    pivot_slices = gather_y(pivot_part)
    disp_slices = gather_y(disp)

    z2 = [send_col(zm[0], 0, 1), send_col(zp[1], 0, -1)]
    xzp = [send_col(zp[0], 1, 0), send_col(xs[1], 0, -1)]
    xzm = [send_col(xs[0], 0, 1), send_col(zm[1], 1, 0)]
    xz2 = [send_col(xzm[0], 0, 1), send_col(xzp[1], 0, -1)]

    def both(piece):
        return piece, send_col(piece, 0, 0, 1)

    first = [[lower_panel, own_other], [lower_panel, own_other]]
    second = [[], []]
    for h in range(2):
        for p in (xs, zm, zp, z2):
            first[h] += both(p[h])
        for p in (xzm, xzp, xz2):
            second[h] += both(p[h])

    offsets = [(dx, dz, dc) for dx, dz in FIRST + SECOND for dc in (0, 1)]
    order = [((x_lo + dx) % 2) * 8 + ((z + dz) % 4) * 2 + (core + dc) % 2 for dx, dz, dc in offsets]
    order = jnp.stack(order + [y]).astype(jnp.int32)

    mine = owned & away
    key = jnp.where(mine, pivots - first_row, jnp.int32(2**30))
    slot_quarter = tops // quarter
    slot_row = ((slot_quarter - y) % 4) * quarter + tops % quarter
    keys, slots, spares = lax.sort((key, slot_row, spare), num_keys=1)
    edges = jnp.arange(local_rows // MB + 1, dtype=jnp.int32) * MB
    starts = jnp.sum((key[None, :] < edges[:, None]).astype(jnp.int32), axis=1)
    info = root.astype(jnp.int32).reshape(1)

    b1h, b1l, b2h, b2l = prep(order, pivot_slices)
    disp_all = jnp.concatenate(disp_slices, axis=0)
    w1, w2 = [True, True] + [False] * 8, [False] * 6
    s1, s2 = (info, starts, keys, spares), (info, starts, keys, slots)
    out = update(first_body, "first_a", 0, s1, first[0], w1, b1h, b1l, matrix, matrix, None)
    out = update(first_body, "first_b", 1, s1, first[1], w1, b1h, b1l, matrix, matrix, out)
    out = update(second_body, "second_a", 0, s2, second[0], w2, b2h, b2l, out, disp_all, out)
    out = update(second_body, "second_b", 1, s2, second[1], w2, b2h, b2l, out, disp_all, out)
    return out


def solution(mesh):
    in_specs = (P("row", "col"), P(), P("col", "row"))
    out_specs = P("row", "col")
    return jax.shard_map(
        per_device, mesh=mesh, in_specs=in_specs, out_specs=out_specs, check_vma=False
    )
```

```python
import functools

import jax
import jax.numpy as jnp
from jax import lax
from jax.experimental import pallas as pl
from jax.experimental.pallas import tpu as pltpu
from jax.sharding import PartitionSpec as P


NZ, NY, NX, NC = 4, 4, 2, 2


def col_shift(dx, dz, dc):
    pairs = []
    for i in range(NX * NZ * NC):
        x, z, c = i // 8, (i // 2) % 4, i % 2
        pairs.append((i, ((x + dx) % 2) * 8 + ((z + dz) % 4) * 2 + (c + dc) % 2))
    return pairs


def row_shift(dx, dy, keep=lambda x: True):
    pairs = []
    for i in range(NX * NY):
        x, y = i // 4, i % 4
        if keep(x):
            pairs.append((i, ((x + dx) % 2) * 4 + (y + dy) % 4))
    return pairs


def send_col(value, dx, dz, dc=0):
    return lax.ppermute(value, "col", col_shift(dx, dz, dc))


def send_row(value, dx, dy, keep=lambda x: True):
    return lax.ppermute(value, "row", row_shift(dx, dy, keep))


FIRST = [(0, 0), (1, 0), (0, -1), (0, 1)]
SECOND = [(0, 2), (1, -1), (1, 1), (1, 2)]
KP = 64
MB = 512


def split(value):
    hi = value.astype(jnp.bfloat16)
    return hi, (value - hi.astype(jnp.float32)).astype(jnp.bfloat16)


def prep_body(order_ref, *refs):
    slices, (b1h, b1l, b2h, b2l), full = refs[:8], refs[8:12], refs[12]
    y = order_ref[16]
    for d in range(4):
        t = lax.rem(y + d, 4)
        for h in range(2):
            full[pl.ds(pl.multiple_of(t * 256 + h * 128, 128), 128), :] = slices[2 * d + h][...]
    n1 = 2 * len(FIRST)
    for j in range(16):
        rows = full[pl.ds(pl.multiple_of(order_ref[j] * KP, KP), KP), :]
        hi, lo = split(rows)
        bh, bl, k = (b1h, b1l, j) if j < n1 else (b2h, b2l, j - n1)
        bh[k * KP : (k + 1) * KP, :] = hi
        bl[k * KP : (k + 1) * KP, :] = lo


def prep(order, slices):
    n = slices[0].shape[1]
    k1, k2 = 2 * len(FIRST) * KP, 2 * len(SECOND) * KP
    out = [jax.ShapeDtypeStruct((k, n), jnp.bfloat16) for k in (k1, k1, k2, k2)]
    vm = pl.BlockSpec(memory_space=pltpu.VMEM)
    return pl.pallas_call(
        prep_body,
        in_specs=[pl.BlockSpec(memory_space=pltpu.SMEM)] + [vm] * len(slices),
        out_specs=[vm] * 4,
        out_shape=out,
        scratch_shapes=[pltpu.VMEM((1024, n), jnp.float32)],
        cost_estimate=pl.CostEstimate(flops=0, bytes_accessed=4 << 20, transcendentals=0),
        name="prep",
    )(order, *slices)


def product(bh, bl, ah, al):
    dot = functools.partial(
        lax.dot_general,
        dimension_numbers=(((0,), (0,)), ((), ())),
        preferred_element_type=jnp.float32,
    )
    return dot(ah[...], bh[...]) + dot(ah[...], bl[...]) + dot(al[...], bh[...])


def load_pieces(pieces, ah, al):
    for j, piece in enumerate(pieces):
        hi, lo = split(piece[...])
        ah[j * KP : (j + 1) * KP, :] = hi
        al[j * KP : (j + 1) * KP, :] = lo


def first_body(info, starts, keys, spares, *refs):
    pieces, (bh, bl, mat, top, out, ah, al) = refs[:8], refs[8:]
    block = pl.program_id(0)
    root = info[0]
    in_top = (root == 1) & (block < 1024 // MB)
    load_pieces(pieces, ah, al)
    out[...] = jnp.where(in_top, 0.0, mat[...])
    lo, hi = starts[block], starts[block + 1]

    @pl.when(root == 1)
    def _():
        def patch(k, carry):
            out[pl.ds(keys[k] - block * MB, 1), :] = top[pl.ds(spares[k], 1), :]
            return carry

        lax.fori_loop(lo, hi, patch, 0)

    @pl.when(root == 0)
    def _():
        def patch(k, carry):
            out[pl.ds(keys[k] - block * MB, 1), :] = jnp.zeros((1, out.shape[1]), jnp.float32)
            return carry

        lax.fori_loop(lo, hi, patch, 0)

    out[...] += jnp.where(in_top, 1.0, -1.0) * product(bh, bl, ah, al)


def second_body(nblk, info, starts, keys, slots, *refs):
    left, right, rest = refs[:8], refs[8:16], refs[16:]
    (bh, bl, prev), parts, (out, ah, al, disp) = rest[:3], rest[3:-4], rest[-4:]
    block = pl.program_id(0)
    root = info[0]
    in_top = (root == 1) & (block < 1024 // MB)

    @pl.when(block == 0)
    def _():
        at = 0
        for part in parts:
            disp[at : at + part.shape[0], :] = part[...]
            at += part.shape[0]

    @pl.when(block < nblk // 2)
    def _():
        load_pieces(left, ah, al)

    @pl.when(block >= nblk // 2)
    def _():
        load_pieces(right, ah, al)

    out[...] = prev[...] + jnp.where(in_top, 1.0, -1.0) * product(bh, bl, ah, al)

    @pl.when(root == 0)
    def _():
        def patch(k, carry):
            out[pl.ds(keys[k] - block * MB, 1), :] += disp[pl.ds(slots[k], 1), :]
            return carry

        lax.fori_loop(starts[block], starts[block + 1], patch, 0)


def const(shape):
    return pl.BlockSpec(shape, lambda i, *_: (0, 0), pipeline_mode=pl.Buffered(1))


def run(body, scalars, pieces, piece_specs, bh, bl, base, extra, scratch, aliases):
    rows, n = base.shape
    k = bh.shape[0]
    return pl.pallas_call(
        body,
        grid_spec=pltpu.PrefetchScalarGridSpec(
            num_scalar_prefetch=4,
            grid=(rows // MB,),
            in_specs=[
                *piece_specs,
                const(bh.shape),
                const(bl.shape),
                pl.BlockSpec((MB, n), lambda i, *_: (i, 0)),
                *[const(e[1]) for e in extra],
            ],
            out_specs=pl.BlockSpec((MB, n), lambda i, *_: (i, 0)),
            scratch_shapes=[pltpu.VMEM((k, MB), jnp.bfloat16)] * 2 + scratch,
        ),
        out_shape=jax.ShapeDtypeStruct(base.shape, jnp.float32),
        input_output_aliases=aliases,
        cost_estimate=pl.CostEstimate(
            flops=6 * rows * n * k, bytes_accessed=4 * (rows * k + 2 * rows * n), transcendentals=0
        ),
    )(*scalars, *pieces, bh, bl, base, *[e[0] for e in extra])


def step(matrix, pivots, lower_panel):
    top = pivots.shape[0]
    local_rows, n = matrix.shape
    row, col = lax.axis_index("row"), lax.axis_index("col")
    x_hi, y = row // 4, row % 4
    x_lo, z, core = col // 8, (col // 2) % 4, col % 2
    first_row = row * local_rows
    root = row == 0
    half = local_rows // 2

    xs = send_col(lower_panel, 1, 0)
    zm = send_col(lower_panel, 0, 1)
    zp = send_col(lower_panel, 0, -1)

    tops = jnp.arange(top, dtype=jnp.int32)
    chosen = jnp.any(pivots[None, :] == tops[:, None], axis=1)
    away = pivots >= top
    rank = jnp.sum((away & (pivots[None, :] < pivots[:, None])).astype(jnp.int32), axis=1)
    before = jnp.sum((~chosen[None, :] & (tops[None, :] < tops[:, None])).astype(jnp.int32), axis=1)
    hit = ~chosen[None, :] & (before[None, :] == rank[:, None])
    spare = jnp.sum(jnp.where(hit, tops[None, :], 0), axis=1)
    owned = (pivots >= first_row) & (pivots < first_row + local_rows)
    index = jnp.where(owned, pivots - first_row, jnp.where(root, spare, 0))
    live = owned | root

    quarter, eighth = top // 4, top // 8

    def gathered(h):
        at = [((y + d) % 4) * quarter + h * eighth for d in (2, 1, 3, 0)]
        idx = jnp.concatenate([lax.dynamic_slice(index, (s,), (eighth,)) for s in at])
        msk = jnp.concatenate([lax.dynamic_slice(live, (s,), (eighth,)) for s in at])
        got = jnp.take(matrix, idx, axis=0, mode="clip")
        got = [jnp.where(msk[i * eighth : (i + 1) * eighth, None], got[i * eighth : (i + 1) * eighth], 0.0) for i in range(4)]
        s = at[3]
        root_owned = (lax.dynamic_slice(pivots, (s,), (eighth,)) < local_rows)[:, None]
        return got, root_owned

    def exchange(got, root_owned):
        m2 = send_row(got[0], 0, 2)
        m1 = send_row(got[1], 0, 1)
        m3 = send_row(got[2], 0, -1)
        pivot_sum, disp = 0.0, 0.0
        for message, source in ((got[3], y), (m1, (y + 3) % 4), (m2, (y + 2) % 4), (m3, (y + 1) % 4)):
            from_root = (x_hi == 0) & (source == 0)
            is_disp = from_root & ~root_owned
            pivot_sum = pivot_sum + jnp.where(is_disp, 0.0, message)
            disp = disp + jnp.where(is_disp, message, 0.0)
        return pivot_sum, disp

    got_a, owned_a = gathered(0)
    got_b, owned_b = gathered(1)
    part_a, disp_a = exchange(got_a, owned_a)
    part_b, disp_b = exchange(got_b, owned_b)
    full_a = part_a + send_row(part_a, 1, 0)
    full_b = part_b + send_row(part_b, 1, 0)
    disp = jnp.concatenate([disp_a, disp_b], axis=0)
    cross = send_row(disp, 1, 0, lambda x: x == 0)
    disp = jnp.where(x_hi == 0, disp, cross)
    lo_a, hi_a = send_row(full_a, 0, 1), send_row(full_a, 0, -1)
    lo_b, hi_b = send_row(full_b, 0, 1), send_row(full_b, 0, -1)
    far_a = send_row(lo_a, 0, 1)
    far_b = send_row(hi_b, 0, -1)
    lo_d, hi_d = send_row(disp, 0, 1), send_row(disp, 0, -1)
    far_da = send_row(lo_d[:eighth], 0, 1)
    far_db = send_row(hi_d[eighth:], 0, -1)
    pivot_slices = [full_a, full_b, hi_a, hi_b, far_a, far_b, lo_a, lo_b]
    disp_parts = [disp, hi_d, far_da, far_db, lo_d]

    up2 = send_col(jnp.concatenate([zm[:, :half], xs[:, :half]], axis=0), 0, 1)
    dn2 = send_col(jnp.concatenate([zp[:, half:], xs[:, half:]], axis=0), 0, -1)
    x2 = send_col(jnp.concatenate([zp[:, :half], zm[:, half:]], axis=0), 1, 0)
    up3 = send_col(up2[KP:], 0, 1)
    dn3 = send_col(dn2[KP:], 0, -1)
    own_o = send_col(lower_panel, 0, 0, 1)
    xs_o, zm_o, zp_o = (send_col(v, 0, 0, 1) for v in (xs, zm, zp))
    x2_o, up2_o, dn2_o = (send_col(v, 0, 0, 1) for v in (x2, up2, dn2))
    up3_o, dn3_o = (send_col(v, 0, 0, 1) for v in (up3, dn3))

    offsets = [(dx, dz, dc) for dx, dz in FIRST + SECOND for dc in (0, 1)]
    order = [((x_lo + dx) % 2) * 8 + ((z + dz) % 4) * 2 + (core + dc) % 2 for dx, dz, dc in offsets]
    order = jnp.stack(order + [y]).astype(jnp.int32)

    mine = owned & away
    key = jnp.where(mine, pivots - first_row, jnp.int32(2**30))
    slot_row = ((tops // quarter - y) % 4) * quarter + tops % quarter
    keys, slots, spares = lax.sort((key, slot_row, spare), num_keys=1)
    edges = jnp.arange(local_rows // MB + 1, dtype=jnp.int32) * MB
    starts = jnp.sum((key[None, :] < edges[:, None]).astype(jnp.int32), axis=1)
    info = root.astype(jnp.int32).reshape(1)

    b1h, b1l, b2h, b2l = prep(order, pivot_slices)
    nblk = local_rows // MB
    hb = nblk // 2
    whole = pl.BlockSpec((KP, MB), lambda i, *_: (0, i))
    out = run(
        first_body, (info, starts, keys, spares),
        [lower_panel, own_o, xs, xs_o, zm, zm_o, zp, zp_o], [whole] * 8,
        b1h, b1l, matrix, [(matrix, (top, n))], [], {},
    )

    def left(r):
        return pl.BlockSpec((KP, MB), lambda i, *_: (r, jnp.minimum(i, hb - 1)))

    def right(r):
        return pl.BlockSpec((KP, MB), lambda i, *_: (r, jnp.maximum(i - hb, 0)))

    pieces = [up2, up2_o, up2, up2_o, x2, x2_o, up3, up3_o]
    specs = [left(r) for r in (0, 0, 1, 1, 0, 0, 0, 0)]
    pieces += [dn2, dn2_o, x2, x2_o, dn2, dn2_o, dn3, dn3_o]
    specs += [right(r) for r in (0, 0, 1, 1, 1, 1, 0, 0)]
    return run(
        functools.partial(second_body, nblk), (info, starts, keys, slots),
        pieces, specs, b2h, b2l, out, [(d, d.shape) for d in disp_parts],
        [pltpu.VMEM((top, n), jnp.float32)], {4 + 16 + 2: 0},
    )


def solution(mesh):
    in_specs = (P("row", "col"), P(), P("col", "row"))
    out_specs = P("row", "col")
    return jax.shard_map(step, mesh=mesh, in_specs=in_specs, out_specs=out_specs, check_vma=False)
```

```python
import functools

import jax
import jax.numpy as jnp
from jax import lax
from jax.experimental import pallas as pl
from jax.experimental.pallas import tpu as pltpu
from jax.sharding import PartitionSpec as P


NZ, NY, NX, NC = 4, 4, 2, 2


def col_shift(dx, dz, dc):
    pairs = []
    for i in range(NX * NZ * NC):
        x, z, c = i // 8, (i // 2) % 4, i % 2
        pairs.append((i, ((x + dx) % 2) * 8 + ((z + dz) % 4) * 2 + (c + dc) % 2))
    return pairs


def row_shift(dx, dy, keep=lambda x: True):
    pairs = []
    for i in range(NX * NY):
        x, y = i // 4, i % 4
        if keep(x):
            pairs.append((i, ((x + dx) % 2) * 4 + (y + dy) % 4))
    return pairs


def send_col(value, dx, dz, dc=0):
    return lax.ppermute(value, "col", col_shift(dx, dz, dc))


def send_row(value, dx, dy, keep=lambda x: True):
    return lax.ppermute(value, "row", row_shift(dx, dy, keep))


PIECES = [(0, 0), (1, 0), (0, -1), (0, 1), (0, 2), (1, -1), (1, 1), (1, 2)]
KP = 64
MB = 512
VMEM = pl.BlockSpec(memory_space=pltpu.VMEM)
ANY = pl.BlockSpec(memory_space=pl.ANY)
SMEM = pl.BlockSpec(memory_space=pltpu.SMEM)


def params(mib):
    return pltpu.CompilerParams(vmem_limit_bytes=mib << 20)


def split(value):
    hi = value.astype(jnp.bfloat16)
    return hi, (value - hi.astype(jnp.float32)).astype(jnp.bfloat16)


def gather_body(h, index, where, matrix, *outs):
    y = where[0]
    for out, d in zip(outs, (2, 1, 3, 0)):
        start = lax.rem(y + d, 4) * 256 + h * 128

        def group(g, carry, out=out, start=start):
            rows = []
            for u in range(8):
                i = index[start + g * 8 + u]
                row = matrix[pl.ds(jnp.maximum(i, 0), 1), :]
                rows.append(jnp.where(i >= 0, row, 0.0))
            out[pl.ds(pl.multiple_of(g * 8, 8), 8), :] = jnp.concatenate(rows, axis=0)
            return carry

        lax.fori_loop(0, 16, group, 0)


def gather_rows(h, index, where, matrix):
    n = matrix.shape[1]
    return pl.pallas_call(
        functools.partial(gather_body, h),
        in_specs=[SMEM, SMEM, VMEM],
        out_specs=[VMEM] * 4,
        out_shape=[jax.ShapeDtypeStruct((128, n), jnp.float32)] * 4,
        compiler_params=params(4),
        cost_estimate=pl.CostEstimate(flops=0, bytes_accessed=6 << 20, transcendentals=0),
        name="gather_rows",
    )(index, where, matrix)


def dots(bh, bl, ah, al):
    dot = functools.partial(
        lax.dot_general,
        dimension_numbers=(((0,), (0,)), ((), ())),
        preferred_element_type=jnp.float32,
    )
    return dot(ah, bh) + dot(ah, bl) + dot(al, bh)


def prep_body(order, *refs):
    slices, (bh, bl), full = refs[:8], refs[8:10], refs[10]
    y = order[16]
    for d in range(4):
        t = lax.rem(y + d, 4)
        for h in range(2):
            full[pl.ds(pl.multiple_of(t * 256 + h * 128, 128), 128), :] = slices[2 * d + h][...]
    for j in range(16):
        rows = full[pl.ds(pl.multiple_of(order[j] * KP, KP), KP), :]
        bh[j * KP : (j + 1) * KP, :], bl[j * KP : (j + 1) * KP, :] = split(rows)


def prep(order, slices):
    n = slices[0].shape[1]
    return pl.pallas_call(
        prep_body,
        in_specs=[SMEM] + [VMEM] * len(slices),
        out_specs=[VMEM] * 2,
        out_shape=[jax.ShapeDtypeStruct((1024, n), jnp.bfloat16)] * 2,
        scratch_shapes=[pltpu.VMEM((1024, n), jnp.float32)],
        compiler_params=params(8),
        cost_estimate=pl.CostEstimate(flops=0, bytes_accessed=4 << 20, transcendentals=0),
        name="prep",
    )(order, *slices)


def update_body(nblk, order, starts, keys, spares, slots, *refs):
    common, left, right = refs[:8], refs[8:16], refs[16:24]
    (bh, bl, base, whole), parts, (out, ah, al, disp, top) = refs[24:28], refs[28:-5], refs[-5:]
    block = pl.program_id(0)
    root = order[17]

    @pl.when(block == 0)
    def _():
        at = 0
        for part in parts:
            disp[at : at + part.shape[0], :] = part[...]
            at += part.shape[0]

    @pl.when((block == 0) & (root == 1))
    def _():
        pltpu.sync_copy(whole.at[pl.ds(0, 1024), :], top)

    def load(first, pieces):
        for j, piece in enumerate(pieces, first):
            ah[j * KP : (j + 1) * KP, :], al[j * KP : (j + 1) * KP, :] = split(piece[...])

    load(0, common)

    @pl.when(block < nblk // 2)
    def _():
        load(8, left)

    @pl.when(block >= nblk // 2)
    def _():
        load(8, right)

    in_top = (root == 1) & (block < 1024 // MB)
    acc = dots(bh[...], bl[...], ah[...], al[...])
    out[...] = jnp.where(in_top, 0.0, base[...]) + jnp.where(in_top, 1.0, -1.0) * acc

    def patch(source, rows):
        def one(k, carry):
            r = pl.ds(keys[k] - block * MB, 1)
            out[r, :] += source[pl.ds(rows[k], 1), :] - base[r, :]
            return carry

        lax.fori_loop(starts[block], starts[block + 1], one, 0)

    @pl.when(root == 1)
    def _():
        patch(top, spares)

    @pl.when(root == 0)
    def _():
        patch(disp, slots)


def update(scalars, common, left, right, cuts_l, cuts_r, bh, bl, matrix, parts):
    rows, n = matrix.shape
    nblk = rows // MB
    hb = nblk // 2

    def const(shape):
        return pl.BlockSpec(shape, lambda i, *_: (0, 0), pipeline_mode=pl.Buffered(1))

    specs = [pl.BlockSpec((KP, MB), lambda i, *_: (0, i))] * 8
    specs += [pl.BlockSpec((KP, MB), lambda i, *_, r=r: (r // KP, jnp.minimum(i, hb - 1))) for r in cuts_l]
    specs += [pl.BlockSpec((KP, MB), lambda i, *_, r=r: (r // KP, jnp.maximum(i - hb, 0))) for r in cuts_r]
    specs += [const(bh.shape), const(bl.shape), pl.BlockSpec((MB, n), lambda i, *_: (i, 0)), ANY]
    specs += [const(p.shape) for p in parts]
    return pl.pallas_call(
        functools.partial(update_body, nblk),
        grid_spec=pltpu.PrefetchScalarGridSpec(
            num_scalar_prefetch=5,
            grid=(nblk,),
            in_specs=specs,
            out_specs=pl.BlockSpec((MB, n), lambda i, *_: (i, 0)),
            scratch_shapes=[pltpu.VMEM((1024, MB), jnp.bfloat16)] * 2 + [pltpu.VMEM((1024, n), jnp.float32)] * 2,
        ),
        out_shape=jax.ShapeDtypeStruct(matrix.shape, jnp.float32),
        compiler_params=params(40),
        cost_estimate=pl.CostEstimate(flops=6 * rows * n * 1024, bytes_accessed=32 << 20, transcendentals=0),
        name="update",
    )(*scalars, *common, *left, *right, bh, bl, matrix, matrix, *parts)


def cut_body(r0, ref, out):
    out[...] = ref[r0 : r0 + out.shape[0], :]


def cut(value, r0, count):
    return pl.pallas_call(
        functools.partial(cut_body, r0),
        in_specs=[VMEM],
        out_specs=VMEM,
        out_shape=jax.ShapeDtypeStruct((count, value.shape[1]), value.dtype),
        compiler_params=params(2),
        cost_estimate=pl.CostEstimate(flops=0, bytes_accessed=1 << 19, transcendentals=0),
        name="cut",
    )(value)


def step(matrix, pivots, lower_panel):
    top = pivots.shape[0]
    local_rows, _ = matrix.shape
    row, col = lax.axis_index("row"), lax.axis_index("col")
    x_hi, y = row // 4, row % 4
    x_lo, z, core = col // 8, (col // 2) % 4, col % 2
    first_row = row * local_rows
    root = row == 0
    half = local_rows // 2

    xs = send_col(lower_panel, 1, 0)
    zm = send_col(lower_panel, 0, 1)
    zp = send_col(lower_panel, 0, -1)

    tops = jnp.arange(top, dtype=jnp.int32)
    chosen = jnp.any(pivots[None, :] == tops[:, None], axis=1)
    away = pivots >= top
    rank = jnp.sum((away & (pivots[None, :] < pivots[:, None])).astype(jnp.int32), axis=1)
    before = jnp.sum((~chosen[None, :] & (tops[None, :] < tops[:, None])).astype(jnp.int32), axis=1)
    hit = ~chosen[None, :] & (before[None, :] == rank[:, None])
    spare = jnp.sum(jnp.where(hit, tops[None, :], 0), axis=1)
    owned = (pivots >= first_row) & (pivots < first_row + local_rows)
    index = jnp.where(owned, pivots - first_row, jnp.where(root, spare, -1))

    quarter, eighth = top // 4, top // 8
    where = y.astype(jnp.int32).reshape(1)
    got_a = gather_rows(0, index, where, matrix)
    got_b = gather_rows(1, index, where, matrix)

    def exchange(h, got):
        root_owned = (lax.dynamic_slice(pivots, (y * quarter + h * eighth,), (eighth,)) < local_rows)[:, None]
        m2 = send_row(got[0], 0, 2)
        m1 = send_row(got[1], 0, 1)
        m3 = send_row(got[2], 0, -1)
        pivot_sum, disp = 0.0, 0.0
        for message, source in ((got[3], y), (m1, (y + 3) % 4), (m2, (y + 2) % 4), (m3, (y + 1) % 4)):
            from_root = (x_hi == 0) & (source == 0)
            is_disp = from_root & ~root_owned
            pivot_sum = pivot_sum + jnp.where(is_disp, 0.0, message)
            disp = disp + jnp.where(is_disp, message, 0.0)
        return pivot_sum, disp

    part_a, disp_a = exchange(0, got_a)
    part_b, disp_b = exchange(1, got_b)
    full_a = part_a + send_row(part_a, 1, 0)
    full_b = part_b + send_row(part_b, 1, 0)
    disp = jnp.concatenate([disp_a, disp_b], axis=0)
    cross = send_row(disp, 1, 0, lambda x: x == 0)
    disp = jnp.where(x_hi == 0, disp, cross)
    lo_a, hi_a = send_row(full_a, 0, 1), send_row(full_a, 0, -1)
    lo_b, hi_b = send_row(full_b, 0, 1), send_row(full_b, 0, -1)
    far_a = send_row(lo_a, 0, 1)
    far_b = send_row(hi_b, 0, -1)
    lo_d, hi_d = send_row(disp, 0, 1), send_row(disp, 0, -1)
    far_da = send_row(cut(lo_d, 0, eighth), 0, 1)
    far_db = send_row(cut(hi_d, eighth, eighth), 0, -1)
    pivot_slices = [full_a, full_b, hi_a, hi_b, far_a, far_b, lo_a, lo_b]
    disp_parts = [disp, hi_d, far_da, far_db, lo_d]

    up2 = send_col(jnp.concatenate([zm[:, :half], xs[:, :half], xs[:, half:]], axis=0), 0, 1)
    dn2 = send_col(jnp.concatenate([zp[:, half:], xs[:, :half], xs[:, half:]], axis=0), 0, -1)
    up3 = send_col(cut(up2, KP, KP), 0, 1)
    dn3 = send_col(cut(dn2, 2 * KP, KP), 0, -1)

    def other(value):
        return send_col(value, 0, 0, 1)

    pairs = [(lower_panel, other(lower_panel)), (xs, other(xs)), (zm, other(zm)), (zp, other(zp))]
    ups, up3s = (up2, other(up2)), (up3, other(up3))
    dns, dn3s = (dn2, other(dn2)), (dn3, other(dn3))

    offsets = [(dx, dz, dc) for dx, dz in PIECES for dc in (0, 1)]
    order = [((x_lo + dx) % 2) * 8 + ((z + dz) % 4) * 2 + (core + dc) % 2 for dx, dz, dc in offsets]
    order = jnp.stack(order + [y, root.astype(jnp.int32)]).astype(jnp.int32)

    mine = owned & away
    key = jnp.where(mine, pivots - first_row, jnp.int32(2**30))
    slot_row = ((tops // quarter - y) % 4) * quarter + tops % quarter
    keys, slots, spares = lax.sort((key, slot_row, spare), num_keys=1)
    edges = jnp.arange(local_rows // MB + 1, dtype=jnp.int32) * MB
    starts = jnp.sum((key[None, :] < edges[:, None]).astype(jnp.int32), axis=1)

    common = [v for pair in pairs for v in pair]
    left = [*ups, *ups, *dns, *up3s]
    right = [*dns, *ups, *dns, *dn3s]
    cuts_l, cuts_r = (0, 0, KP, KP, KP, KP, 0, 0), (0, 0, 2 * KP, 2 * KP, 2 * KP, 2 * KP, 0, 0)
    bh, bl = prep(order, pivot_slices)
    return update((order, starts, keys, spares, slots), common, left, right, cuts_l, cuts_r, bh, bl, matrix, disp_parts)


def solution(mesh):
    in_specs = (P("row", "col"), P(), P("col", "row"))
    out_specs = P("row", "col")
    return jax.shard_map(step, mesh=mesh, in_specs=in_specs, out_specs=out_specs, check_vma=False)
```

```python
import functools

import jax
import jax.numpy as jnp
from jax import lax
from jax.experimental import pallas as pl
from jax.experimental.pallas import tpu as pltpu
from jax.sharding import PartitionSpec as P


NZ, NY, NX, NC = 4, 4, 2, 2


def torus(step):
    pairs = []
    for r in range(NX * NY):
        for q in range(NX * NZ * NC):
            xh, y, xl, z, c = step(r // 4, r % 4, q // 8, (q // 2) % 4, q % 2)
            pairs.append((r * 16 + q, ((xh % 2) * 4 + y % 4) * 16 + (xl % 2) * 8 + (z % 4) * 2 + c % 2))
    return pairs


def send(value, step):
    return lax.ppermute(value, ("row", "col"), torus(step))


def way(c):
    return 1 if c == 0 else -1


def z_way(xh, y, xl, z, c):
    return xh, y, xl, z + way(c), c


def z_back(xh, y, xl, z, c):
    return xh, y, xl, z - way(c), c


def y_way(xh, y, xl, z, c):
    return xh, y + way(c), xl, z, c


def y_back(xh, y, xl, z, c):
    return xh, y - way(c), xl, z, c


def x_lo_swap(xh, y, xl, z, c):
    return xh, y, 1 - xl, z, c


def x_hi_swap(xh, y, xl, z, c):
    return 1 - xh, y, xl, z, c


def core_swap(xh, y, xl, z, c):
    return xh, y, xl, z, 1 - c


def row_pairs(dx, dy, keep=lambda x: True):
    return [(i, ((i // 4 + dx) % 2) * 4 + (i + dy) % 4) for i in range(NX * NY) if keep(i // 4)]


def send_row(value, dx, dy, keep=lambda x: True):
    return lax.ppermute(value, "row", row_pairs(dx, dy, keep))


KP = 64
MB = 512
VMEM = pl.BlockSpec(memory_space=pltpu.VMEM)
ANY = pl.BlockSpec(memory_space=pl.ANY)
SMEM = pl.BlockSpec(memory_space=pltpu.SMEM)


def params(mib):
    return pltpu.CompilerParams(vmem_limit_bytes=mib << 20)


def split(value):
    hi = value.astype(jnp.bfloat16)
    return hi, (value - hi.astype(jnp.float32)).astype(jnp.bfloat16)


def index_body(where, p_ref, index, spare_ref):
    first, root = where[1], where[2]
    p = p_ref[...]
    top = p.shape[1]
    side = 128
    sub = lax.broadcasted_iota(jnp.int32, (side, top), 0)
    lane = lax.broadcasted_iota(jnp.int32, (1, top), 1)

    def column(line, c):
        square = jnp.broadcast_to(line[:, c * side : (c + 1) * side], (side, side)).T
        return jnp.concatenate([square] * (top // side), axis=1)

    def count(hits):
        return jnp.sum(hits, axis=0, keepdims=True)

    chosen = jnp.zeros((1, top), jnp.int32)
    rank = jnp.zeros((1, top), jnp.int32)
    for c in range(top // side):
        pc = column(p, c)
        chosen += count(jnp.where(pc == lane, 1, 0))
        rank += count(jnp.where((pc >= top) & (pc < p), 1, 0))
    free = jnp.where(chosen == 0, 1.0, 0.0)
    before = jnp.zeros((8, top), jnp.float32)
    for c in range(top // side):
        ahead = jnp.where(sub + c * side < lane, 1.0, 0.0).astype(jnp.bfloat16)
        some = jnp.broadcast_to(free[:, c * side : (c + 1) * side], (8, side)).astype(jnp.bfloat16)
        before += jnp.dot(some, ahead, preferred_element_type=jnp.float32)
    place = jnp.where(chosen == 0, before[0:1].astype(jnp.int32), -1)
    spare = jnp.zeros((1, top), jnp.int32)
    for c in range(top // side):
        spare += count(jnp.where(column(place, c) == rank, sub + c * side, 0))
    local = p - first
    owned = (local >= 0) & (local < where[3])
    index[...] = jnp.where(owned, local, jnp.where(root == 1, spare, -1))
    spare_ref[...] = spare


def row_index(where, line):
    shape = jax.ShapeDtypeStruct(line.shape, jnp.int32)
    return pl.pallas_call(
        index_body,
        in_specs=[SMEM, VMEM],
        out_specs=[VMEM] * 2,
        out_shape=[shape] * 2,
        compiler_params=params(6),
        cost_estimate=pl.CostEstimate(flops=0, bytes_accessed=1 << 20, transcendentals=0),
        name="row_index",
    )(where, line)


def gather_body(h, index, where, matrix, *outs):
    y = where[0]
    for out, d in zip(outs, (2, 1, 3, 0)):
        start = lax.rem(y + d, 4) * 256 + h * 128

        def group(g, carry, out=out, start=start):
            rows = []
            for u in range(8):
                i = index[0, start + g * 8 + u]
                row = matrix[pl.ds(jnp.maximum(i, 0), 1), :]
                rows.append(jnp.where(i >= 0, row, 0.0))
            out[pl.ds(pl.multiple_of(g * 8, 8), 8), :] = jnp.concatenate(rows, axis=0)
            return carry

        lax.fori_loop(0, 16, group, 0)


def gather_rows(h, index, where, matrix):
    n = matrix.shape[1]
    return pl.pallas_call(
        functools.partial(gather_body, h),
        in_specs=[SMEM, SMEM, VMEM],
        out_specs=[VMEM] * 4,
        out_shape=[jax.ShapeDtypeStruct((128, n), jnp.float32)] * 4,
        compiler_params=params(4),
        cost_estimate=pl.CostEstimate(flops=0, bytes_accessed=6 << 20, transcendentals=0),
        name="gather_rows",
    )(index, where, matrix)


def dots(bh, bl, ah, al):
    dot = functools.partial(
        lax.dot_general,
        dimension_numbers=(((0,), (0,)), ((), ())),
        preferred_element_type=jnp.float32,
    )
    return dot(ah, bh) + dot(ah, bl) + dot(al, bh)


def prep_body(order, *refs):
    slices, (bh, bl), full = refs[:8], refs[8:10], refs[10]
    y, da = order[16], order[18]
    for s, d in enumerate((0, da, 4 - da, 2)):
        t = lax.rem(y + d, 4)
        for h in range(2):
            full[pl.ds(pl.multiple_of(t * 256 + h * 128, 128), 128), :] = slices[2 * s + h][...]
    for j in range(16):
        rows = full[pl.ds(pl.multiple_of(order[j] * KP, KP), KP), :]
        bh[j * KP : (j + 1) * KP, :], bl[j * KP : (j + 1) * KP, :] = split(rows)


def prep(order, slices):
    n = slices[0].shape[1]
    return pl.pallas_call(
        prep_body,
        in_specs=[SMEM] + [VMEM] * len(slices),
        out_specs=[VMEM] * 2,
        out_shape=[jax.ShapeDtypeStruct((1024, n), jnp.bfloat16)] * 2,
        scratch_shapes=[pltpu.VMEM((1024, n), jnp.float32)],
        compiler_params=params(8),
        cost_estimate=pl.CostEstimate(flops=0, bytes_accessed=4 << 20, transcendentals=0),
        name="prep",
    )(order, *slices)


def load(first, pieces, into=None):
    m = pieces[0].shape[1]
    n = len(pieces)

    def body(*refs):
        ah, al = refs[-2:]

        def block_step(*io):
            at = pl.ds(pl.multiple_of(pl.program_id(0) * MB, MB), MB)
            for j, piece in enumerate(io, first):
                ah[j * KP : (j + 1) * KP, at], al[j * KP : (j + 1) * KP, at] = split(piece[...])

        if into is not None:
            for j, piece in enumerate(refs[:n], first):
                ah[j * KP : (j + 1) * KP, :], al[j * KP : (j + 1) * KP, :] = split(piece[...])
            return
        spec = pl.BlockSpec((KP, MB), lambda i: (0, i))
        pltpu.emit_pipeline(block_step, grid=(m // MB,), in_specs=[spec] * n)(*refs[:n])

    return pl.pallas_call(
        body,
        in_specs=[ANY] * n if into is None else [VMEM] * (n + 2),
        out_specs=[VMEM] * 2,
        out_shape=[jax.ShapeDtypeStruct((16 * KP, m), jnp.bfloat16)] * 2,
        input_output_aliases={} if into is None else {n: 0, n + 1: 1},
        compiler_params=params(12),
        cost_estimate=pl.CostEstimate(flops=0, bytes_accessed=n << 20, transcendentals=0),
    )(*pieces, *([] if into is None else into))


def update(scalars, panel, bh, bl, matrix, parts):
    rows, n = matrix.shape
    nblk = rows // MB

    def body(order, starts, keys, spares, slots, ph, pw, bh, bl, matrix, *refs):
        parts, (out, disp) = refs[:4], refs[4:]
        root = order[17]
        for i, part in enumerate(parts):
            disp[i * 256 : (i + 1) * 256, :] = part[...]

        def block_step(dest):
            block = pl.program_id(0)
            at = pl.ds(pl.multiple_of(block * MB, MB), MB)
            in_top = (root == 1) & (block < 1024 // MB)
            acc = dots(bh[...], bl[...], ph[:, at], pw[:, at])
            dest[...] = jnp.where(in_top, 0.0, matrix[at, :]) + jnp.where(in_top, 1.0, -1.0) * acc

            def patch(source, rows_of):
                def one(k, carry):
                    r = keys[k]
                    dest[pl.ds(r - block * MB, 1), :] += source[pl.ds(rows_of[k], 1), :] - matrix[pl.ds(r, 1), :]
                    return carry

                lax.fori_loop(starts[block], starts[block + 1], one, 0)

            @pl.when(root == 1)
            def _():
                patch(matrix, spares)

            @pl.when(root == 0)
            def _():
                patch(disp, slots)

        pltpu.emit_pipeline(
            block_step, grid=(nblk,), in_specs=[], out_specs=[pl.BlockSpec((MB, n), lambda i: (i, 0))]
        )(out)

    return pl.pallas_call(
        body,
        in_specs=[SMEM] * 5 + [VMEM] * 9,
        out_specs=ANY,
        out_shape=jax.ShapeDtypeStruct(matrix.shape, jnp.float32),
        scratch_shapes=[pltpu.VMEM((1024, n), jnp.float32)],
        compiler_params=params(14),
        cost_estimate=pl.CostEstimate(flops=6 * rows * n * 1024, bytes_accessed=8 << 20, transcendentals=0),
        name="update",
    )(*scalars, *panel, bh, bl, matrix, *parts)


def step(matrix, pivots, lower_panel):
    top = pivots.shape[0]
    local_rows, _ = matrix.shape
    row, col = lax.axis_index("row"), lax.axis_index("col")
    x_hi, y = row // 4, row % 4
    x_lo, z, core = col // 8, (col // 2) % 4, col % 2
    first_row = row * local_rows
    root = row == 0
    quarter, eighth = top // 4, top // 8

    own = lower_panel
    xs = send(own, x_lo_swap)
    za = send(own, z_way)
    zb = send(own, z_back)
    xa = send(xs, z_way)
    xb = send(xs, z_back)
    z2 = send(za, z_way)
    x2 = send(xa, z_way)
    pieces = []
    for piece in (own, xs, za, zb, xa, xb, z2, x2):
        pieces += [piece, send(piece, core_swap)]

    where = jnp.stack([y, first_row, root.astype(jnp.int32), jnp.int32(local_rows)]).astype(jnp.int32)
    index, spare = row_index(where, pivots.reshape(1, top))

    got_a = gather_rows(0, index, where, matrix)
    got_b = gather_rows(1, index, where, matrix)

    def exchange(h, got):
        root_owned = (lax.dynamic_slice(pivots, (y * quarter + h * eighth,), (eighth,)) < local_rows)[:, None]
        m2 = send_row(got[0], 0, 2)
        m1 = send_row(got[1], 0, 1)
        m3 = send_row(got[2], 0, -1)
        pivot_sum, disp = 0.0, 0.0
        for message, source in ((got[3], y), (m1, (y + 3) % 4), (m2, (y + 2) % 4), (m3, (y + 1) % 4)):
            from_root = (x_hi == 0) & (source == 0)
            is_disp = from_root & ~root_owned
            pivot_sum = pivot_sum + jnp.where(is_disp, 0.0, message)
            disp = disp + jnp.where(is_disp, message, 0.0)
        return pivot_sum, disp

    part_a, disp_a = exchange(0, got_a)
    part_b, disp_b = exchange(1, got_b)
    disp = jnp.concatenate([disp_a, disp_b], axis=0)
    full_a = part_a + send(part_a, x_hi_swap)
    full_b = part_b + send(part_b, x_hi_swap)
    cross = send_row(disp, 1, 0, lambda x: x == 0)
    disp = jnp.where(x_hi == 0, disp, cross)
    a_a, b_a = send(full_a, y_way), send(full_a, y_back)
    a_b, b_b = send(full_b, y_way), send(full_b, y_back)
    f_a, f_b = send(a_a, y_way), send(a_b, y_way)
    a_d, b_d = send(disp, y_way), send(disp, y_back)
    f_d = send(a_d, y_way)
    a_off = jnp.where(core == 0, 3, 1)

    dz = jnp.where(core == 0, -1, 1)

    def block(dx, dzs, dc):
        return ((x_lo + dx) % 2) * 8 + ((z + dzs + 4) % 4) * 2 + (core + dc) % 2

    order = []
    for dx, sign in ((0, 0), (1, 0), (0, 1), (0, -1), (1, 1), (1, -1), (0, 2), (1, 2)):
        order += [block(dx, sign * dz, 0), block(dx, -sign * dz, 1)]
    order = jnp.stack(order + [y, root.astype(jnp.int32), a_off]).astype(jnp.int32)

    owned = (pivots >= first_row) & (pivots < first_row + local_rows)
    key = jnp.where(owned & (pivots >= top), pivots - first_row, jnp.int32(2**30))
    slot = jnp.arange(top, dtype=jnp.int32)
    off = (slot // quarter - y + 4) % 4
    part = jnp.where(off == 0, 0, jnp.where(off == 2, 3, jnp.where(off == a_off, 1, 2)))
    keys, slots, spares = lax.sort((key, part * quarter + slot % quarter, spare.reshape(top)), num_keys=1)
    edges = jnp.arange(local_rows // MB + 1, dtype=jnp.int32) * MB
    starts = jnp.sum((key[None, :] < edges[:, None]).astype(jnp.int32), axis=1)

    bh, bl = prep(order, [full_a, full_b, a_a, a_b, b_a, b_b, f_a, f_b])
    panel = load(0, pieces[:14])
    panel = load(14, pieces[14:], panel)
    return update((order, starts, keys, spares, slots), panel, bh, bl, matrix, [disp, a_d, b_d, f_d])


def solution(mesh):
    in_specs = (P("row", "col"), P(), P("col", "row"))
    out_specs = P("row", "col")
    return jax.shard_map(step, mesh=mesh, in_specs=in_specs, out_specs=out_specs, check_vma=False)
```

```python
import functools

import jax
import jax.numpy as jnp
from jax import lax
from jax.experimental import pallas as pl
from jax.experimental.pallas import tpu as pltpu
from jax.sharding import PartitionSpec as P


NZ, NY, NX, NC = 4, 4, 2, 2


def torus(step):
    pairs = []
    for r in range(NX * NY):
        for q in range(NX * NZ * NC):
            xh, y, xl, z, c = step(r // 4, r % 4, q // 8, (q // 2) % 4, q % 2)
            pairs.append((r * 16 + q, ((xh % 2) * 4 + y % 4) * 16 + (xl % 2) * 8 + (z % 4) * 2 + c % 2))
    return pairs


def send(value, step):
    return lax.ppermute(value, ("row", "col"), torus(step))


def way(c):
    return 1 if c == 0 else -1


def z_way(xh, y, xl, z, c):
    return xh, y, xl, z + way(c), c


def z_back(xh, y, xl, z, c):
    return xh, y, xl, z - way(c), c


def y_way(xh, y, xl, z, c):
    return xh, y + way(c), xl, z, c


def y_back(xh, y, xl, z, c):
    return xh, y - way(c), xl, z, c


def x_lo_swap(xh, y, xl, z, c):
    return xh, y, 1 - xl, z, c


def x_hi_swap(xh, y, xl, z, c):
    return 1 - xh, y, xl, z, c


def core_swap(xh, y, xl, z, c):
    return xh, y, xl, z, 1 - c


def row_pairs(dx, dy, keep=lambda x: True):
    return [(i, ((i // 4 + dx) % 2) * 4 + (i + dy) % 4) for i in range(NX * NY) if keep(i // 4)]


def send_row(value, dx, dy, keep=lambda x: True):
    return lax.ppermute(value, "row", row_pairs(dx, dy, keep))


KP = 64
MB = 512
VMEM = pl.BlockSpec(memory_space=pltpu.VMEM)
ANY = pl.BlockSpec(memory_space=pl.ANY)
SMEM = pl.BlockSpec(memory_space=pltpu.SMEM)
HBM = pl.BlockSpec(memory_space=pltpu.HBM)


def params(mib):
    return pltpu.CompilerParams(vmem_limit_bytes=mib << 20)


def split(value):
    hi = value.astype(jnp.bfloat16)
    return hi, (value - hi.astype(jnp.float32)).astype(jnp.bfloat16)


def index_body(where, p_ref, index, spare_ref):
    first, root = where[1], where[2]
    p = p_ref[...]
    top = p.shape[1]
    side = 128
    sub = lax.broadcasted_iota(jnp.int32, (side, top), 0)
    lane = lax.broadcasted_iota(jnp.int32, (1, top), 1)

    def column(line, c):
        square = jnp.broadcast_to(line[:, c * side : (c + 1) * side], (side, side)).T
        return jnp.concatenate([square] * (top // side), axis=1)

    def count(hits):
        return jnp.sum(hits, axis=0, keepdims=True)

    chosen = jnp.zeros((1, top), jnp.int32)
    rank = jnp.zeros((1, top), jnp.int32)
    for c in range(top // side):
        pc = column(p, c)
        chosen += count(jnp.where(pc == lane, 1, 0))
        rank += count(jnp.where((pc >= top) & (pc < p), 1, 0))
    free = jnp.where(chosen == 0, 1.0, 0.0)
    before = jnp.zeros((8, top), jnp.float32)
    for c in range(top // side):
        ahead = jnp.where(sub + c * side < lane, 1.0, 0.0).astype(jnp.bfloat16)
        some = jnp.broadcast_to(free[:, c * side : (c + 1) * side], (8, side)).astype(jnp.bfloat16)
        before += jnp.dot(some, ahead, preferred_element_type=jnp.float32)
    place = jnp.where(chosen == 0, before[0:1].astype(jnp.int32), -1)
    spare = jnp.zeros((1, top), jnp.int32)
    for c in range(top // side):
        spare += count(jnp.where(column(place, c) == rank, sub + c * side, 0))
    local = p - first
    owned = (local >= 0) & (local < where[3])
    index[...] = jnp.where(owned, local, jnp.where(root == 1, spare, -1))
    spare_ref[...] = spare


def row_index(where, line):
    shape = jax.ShapeDtypeStruct(line.shape, jnp.int32)
    return pl.pallas_call(
        index_body,
        in_specs=[SMEM, VMEM],
        out_specs=[VMEM] * 2,
        out_shape=[shape] * 2,
        compiler_params=params(6),
        cost_estimate=pl.CostEstimate(flops=6 << 30, bytes_accessed=1 << 20, transcendentals=0),
        name="row_index",
    )(where, line)


def gather_body(h, index, where, matrix, *outs):
    y = where[0]
    for out, d in zip(outs, (2, 1, 3, 0)):
        start = lax.rem(y + d, 4) * 256 + h * 128

        def group(g, carry, out=out, start=start):
            rows = []
            for u in range(8):
                i = index[0, start + g * 8 + u]
                row = matrix[pl.ds(jnp.maximum(i, 0), 1), :]
                rows.append(jnp.where(i >= 0, row, 0.0))
            out[pl.ds(pl.multiple_of(g * 8, 8), 8), :] = jnp.concatenate(rows, axis=0)
            return carry

        lax.fori_loop(0, 16, group, 0)


def gather_rows(h, index, where, matrix):
    n = matrix.shape[1]
    return pl.pallas_call(
        functools.partial(gather_body, h),
        in_specs=[SMEM, SMEM, VMEM],
        out_specs=[VMEM] * 4,
        out_shape=[jax.ShapeDtypeStruct((128, n), jnp.float32)] * 4,
        compiler_params=params(4),
        cost_estimate=pl.CostEstimate(flops=0, bytes_accessed=6 << 20, transcendentals=0),
        name="gather_rows",
    )(index, where, matrix)


def dots(bh, bl, ah, al):
    dot = functools.partial(
        lax.dot_general,
        dimension_numbers=(((0,), (0,)), ((), ())),
        preferred_element_type=jnp.float32,
    )
    return dot(ah, bh) + dot(ah, bl) + dot(al, bh)


def prep_body(order, *refs):
    slices, (bh, bl), full = refs[:8], refs[8:10], refs[10]
    y, da = order[16], order[18]
    for s, d in enumerate((0, da, 4 - da, 2)):
        t = lax.rem(y + d, 4)
        for h in range(2):
            full[pl.ds(pl.multiple_of(t * 256 + h * 128, 128), 128), :] = slices[2 * s + h][...]
    for j in range(16):
        rows = full[pl.ds(pl.multiple_of(order[j] * KP, KP), KP), :]
        bh[j * KP : (j + 1) * KP, :], bl[j * KP : (j + 1) * KP, :] = split(rows)


def prep(order, slices):
    n = slices[0].shape[1]
    return pl.pallas_call(
        prep_body,
        in_specs=[SMEM] + [VMEM] * len(slices),
        out_specs=[VMEM] * 2,
        out_shape=[jax.ShapeDtypeStruct((1024, n), jnp.bfloat16)] * 2,
        scratch_shapes=[pltpu.VMEM((1024, n), jnp.float32)],
        compiler_params=params(8),
        cost_estimate=pl.CostEstimate(flops=0, bytes_accessed=4 << 20, transcendentals=0),
        name="prep",
    )(order, *slices)


def load(first, pieces, into=None):
    m = pieces[0].shape[1]
    n = len(pieces)

    def body(*refs):
        ah, al = refs[-2:]

        def block_step(*io):
            at = pl.ds(pl.multiple_of(pl.program_id(0) * MB, MB), MB)
            for j, piece in enumerate(io, first):
                ah[j * KP : (j + 1) * KP, at], al[j * KP : (j + 1) * KP, at] = split(piece[...])

        if into is not None:
            for j, piece in enumerate(refs[:n], first):
                ah[j * KP : (j + 1) * KP, :], al[j * KP : (j + 1) * KP, :] = split(piece[...])
            return
        spec = pl.BlockSpec((KP, MB), lambda i: (0, i))
        pltpu.emit_pipeline(block_step, grid=(m // MB,), in_specs=[spec] * n)(*refs[:n])

    return pl.pallas_call(
        body,
        in_specs=[HBM] + [ANY] * (n - 1) if into is None else [VMEM] * (n + 2),
        out_specs=[VMEM] * 2,
        out_shape=[jax.ShapeDtypeStruct((16 * KP, m), jnp.bfloat16)] * 2,
        input_output_aliases={} if into is None else {n: 0, n + 1: 1},
        compiler_params=params(12),
        cost_estimate=pl.CostEstimate(flops=0, bytes_accessed=n << 20, transcendentals=0),
    )(*pieces, *([] if into is None else into))


def update_left(scalars, panel, bh, bl, matrix):
    rows, n = matrix.shape
    half = rows // 2

    def body(order, starts, keys, spares, ph, pw, bh, bl, matrix, out):
        root = order[17]

        def block_step(block, carry):
            at = pl.ds(pl.multiple_of(block * MB, MB), MB)
            in_top = (root == 1) & (block < 1024 // MB)
            acc = dots(bh[...], bl[...], ph[:, at], pw[:, at])
            out[at, :] = jnp.where(in_top, 0.0, matrix[at, :]) + jnp.where(in_top, 1.0, -1.0) * acc
            return carry

        lax.fori_loop(0, half // MB, block_step, 0)

        def patch(k, carry):
            r = pl.ds(keys[k], 1)
            line = jnp.where(root == 1, matrix[pl.ds(spares[k], 1), :], 0.0)
            out[r, :] += line - matrix[r, :]
            return carry

        lax.fori_loop(0, starts[half // MB], patch, 0)

    return pl.pallas_call(
        body,
        in_specs=[SMEM] * 4 + [VMEM] * 5,
        out_specs=VMEM,
        out_shape=jax.ShapeDtypeStruct((half, n), jnp.float32),
        compiler_params=params(14),
        cost_estimate=pl.CostEstimate(flops=3 * rows * n * 1024, bytes_accessed=1 << 20, transcendentals=0),
        name="update_left",
    )(*scalars, *panel, bh, bl, matrix)


def update_right(scalars, panel, bh, bl, matrix, left, parts):
    rows, n = matrix.shape
    first = rows // 2 // MB

    def body(order, starts, keys, spares, slots, ph, pw, bh, bl, matrix, _, *refs):
        parts, (out, left, disp, sem) = refs[:4], refs[4:]
        root = order[17]
        for i, part in enumerate(parts):
            disp[i * 256 : (i + 1) * 256, :] = part[...]

        @pl.when(root == 0)
        def _():
            def one(k, carry):
                left[pl.ds(keys[k], 1), :] += disp[pl.ds(slots[k], 1), :]
                return carry

            lax.fori_loop(0, starts[first], one, 0)

        away = pltpu.make_async_copy(left, out.at[pl.ds(0, first * MB), :], sem)
        away.start()

        def block_step(dest):
            block = pl.program_id(0) + first
            at = pl.ds(pl.multiple_of(block * MB, MB), MB)
            dest[...] = matrix[at, :] - dots(bh[...], bl[...], ph[:, at], pw[:, at])

            def patch(source, rows_of):
                def one(k, carry):
                    r = keys[k]
                    dest[pl.ds(r - block * MB, 1), :] += source[pl.ds(rows_of[k], 1), :] - matrix[pl.ds(r, 1), :]
                    return carry

                lax.fori_loop(starts[block], starts[block + 1], one, 0)

            @pl.when(root == 1)
            def _():
                patch(matrix, spares)

            @pl.when(root == 0)
            def _():
                patch(disp, slots)

        pltpu.emit_pipeline(
            block_step, grid=(first,), in_specs=[], out_specs=[pl.BlockSpec((MB, n), lambda i: (i + first, 0))]
        )(out)
        away.wait()

    return pl.pallas_call(
        body,
        in_specs=[SMEM] * 5 + [VMEM] * 10,
        out_specs=[ANY, VMEM],
        out_shape=[jax.ShapeDtypeStruct(matrix.shape, jnp.float32), jax.ShapeDtypeStruct(left.shape, jnp.float32)],
        scratch_shapes=[pltpu.VMEM((1024, n), jnp.float32), pltpu.SemaphoreType.DMA],
        input_output_aliases={10: 1},
        compiler_params=params(14),
        cost_estimate=pl.CostEstimate(flops=3 * rows * n * 1024, bytes_accessed=8 << 20, transcendentals=0),
        name="update_right",
    )(*scalars, *panel, bh, bl, matrix, left, *parts)[0]


def step(matrix, pivots, lower_panel):
    top = pivots.shape[0]
    local_rows, _ = matrix.shape
    row, col = lax.axis_index("row"), lax.axis_index("col")
    x_hi, y = row // 4, row % 4
    x_lo, z, core = col // 8, (col // 2) % 4, col % 2
    first_row = row * local_rows
    root = row == 0
    quarter, eighth = top // 4, top // 8

    own = lower_panel
    xs = send(own, x_lo_swap)
    za = send(own, z_way)
    zb = send(own, z_back)
    xa = send(xs, z_way)
    xb = send(xs, z_back)
    z2 = send(za, z_way)
    x2 = send(xa, z_way)
    pieces = []
    for piece in (own, xs, za, zb, xa, xb, z2, x2):
        pieces += [piece, send(piece, core_swap)]

    where = jnp.stack([y, first_row, root.astype(jnp.int32), jnp.int32(local_rows)]).astype(jnp.int32)
    index, spare = row_index(where, pivots.reshape(1, top))

    got_a = gather_rows(0, index, where, matrix)
    got_b = gather_rows(1, index, where, matrix)

    def exchange(h, got):
        root_owned = (lax.dynamic_slice(pivots, (y * quarter + h * eighth,), (eighth,)) < local_rows)[:, None]
        m2 = send_row(got[0], 0, 2)
        m1 = send_row(got[1], 0, 1)
        m3 = send_row(got[2], 0, -1)
        pivot_sum, disp = 0.0, 0.0
        for message, source in ((got[3], y), (m1, (y + 3) % 4), (m2, (y + 2) % 4), (m3, (y + 1) % 4)):
            from_root = (x_hi == 0) & (source == 0)
            is_disp = from_root & ~root_owned
            pivot_sum = pivot_sum + jnp.where(is_disp, 0.0, message)
            disp = disp + jnp.where(is_disp, message, 0.0)
        return pivot_sum, disp

    part_a, disp_a = exchange(0, got_a)
    part_b, disp_b = exchange(1, got_b)
    disp = jnp.concatenate([disp_a, disp_b], axis=0)
    full_a = part_a + send(part_a, x_hi_swap)
    full_b = part_b + send(part_b, x_hi_swap)
    cross = send_row(disp, 1, 0, lambda x: x == 0)
    disp = jnp.where(x_hi == 0, disp, cross)
    a_a, b_a = send(full_a, y_way), send(full_a, y_back)
    a_b, b_b = send(full_b, y_way), send(full_b, y_back)
    f_a, f_b = send(a_a, y_way), send(a_b, y_way)
    a_d, b_d = send(disp, y_way), send(disp, y_back)
    f_d = send(a_d, y_way)
    a_off = jnp.where(core == 0, 3, 1)

    dz = jnp.where(core == 0, -1, 1)

    def block(dx, dzs, dc):
        return ((x_lo + dx) % 2) * 8 + ((z + dzs + 4) % 4) * 2 + (core + dc) % 2

    order = []
    for dx, sign in ((0, 0), (1, 0), (0, 1), (0, -1), (1, 1), (1, -1), (0, 2), (1, 2)):
        order += [block(dx, sign * dz, 0), block(dx, -sign * dz, 1)]
    order = jnp.stack(order + [y, root.astype(jnp.int32), a_off]).astype(jnp.int32)

    owned = (pivots >= first_row) & (pivots < first_row + local_rows)
    key = jnp.where(owned & (pivots >= top), pivots - first_row, jnp.int32(2**30))
    slot = jnp.arange(top, dtype=jnp.int32)
    off = (slot // quarter - y + 4) % 4
    part = jnp.where(off == 0, 0, jnp.where(off == 2, 3, jnp.where(off == a_off, 1, 2)))
    keys, slots, spares = lax.sort((key, part * quarter + slot % quarter, spare.reshape(top)), num_keys=1)
    edges = jnp.arange(local_rows // MB + 1, dtype=jnp.int32) * MB
    starts = jnp.sum((key[None, :] < edges[:, None]).astype(jnp.int32), axis=1)

    bh, bl = prep(order, [full_a, full_b, a_a, a_b, b_a, b_b, f_a, f_b])
    panel = load(0, pieces[:14])
    panel = load(14, pieces[14:], panel)
    left = update_left((order, starts, keys, spares), panel, bh, bl, matrix)
    return update_right((order, starts, keys, spares, slots), panel, bh, bl, matrix, left, [disp, a_d, b_d, f_d])


def solution(mesh):
    in_specs = (P("row", "col"), P(), P("col", "row"))
    out_specs = P("row", "col")
    return jax.shard_map(step, mesh=mesh, in_specs=in_specs, out_specs=out_specs, check_vma=False)
```

```python
import functools

import jax
import jax.numpy as jnp
from jax import lax
from jax.experimental import pallas as pl
from jax.experimental.pallas import tpu as pltpu
from jax.sharding import PartitionSpec as P


NZ, NY, NX, NC = 4, 4, 2, 2


def torus(step):
    pairs = []
    for r in range(NX * NY):
        for q in range(NX * NZ * NC):
            xh, y, xl, z, c = step(r // 4, r % 4, q // 8, (q // 2) % 4, q % 2)
            pairs.append((r * 16 + q, ((xh % 2) * 4 + y % 4) * 16 + (xl % 2) * 8 + (z % 4) * 2 + c % 2))
    return pairs


def send(value, step):
    return lax.ppermute(value, ("row", "col"), torus(step))


def way(c):
    return 1 if c == 0 else -1


def z_way(xh, y, xl, z, c):
    return xh, y, xl, z + way(c), c


def z_back(xh, y, xl, z, c):
    return xh, y, xl, z - way(c), c


def y_way(xh, y, xl, z, c):
    return xh, y + way(c), xl, z, c


def y_back(xh, y, xl, z, c):
    return xh, y - way(c), xl, z, c


def x_lo_swap(xh, y, xl, z, c):
    return xh, y, 1 - xl, z, c


def x_hi_swap(xh, y, xl, z, c):
    return 1 - xh, y, xl, z, c


def core_swap(xh, y, xl, z, c):
    return xh, y, xl, z, 1 - c


def row_pairs(dx, dy, keep=lambda x: True):
    return [(i, ((i // 4 + dx) % 2) * 4 + (i + dy) % 4) for i in range(NX * NY) if keep(i // 4)]


def send_row(value, dx, dy, keep=lambda x: True):
    return lax.ppermute(value, "row", row_pairs(dx, dy, keep))


KP = 64
MB = 512
VMEM = pl.BlockSpec(memory_space=pltpu.VMEM)
ANY = pl.BlockSpec(memory_space=pl.ANY)
SMEM = pl.BlockSpec(memory_space=pltpu.SMEM)
HBM = pl.BlockSpec(memory_space=pltpu.HBM)


def params(mib):
    return pltpu.CompilerParams(vmem_limit_bytes=mib << 20)


def split(value):
    hi = value.astype(jnp.bfloat16)
    return hi, (value - hi.astype(jnp.float32)).astype(jnp.bfloat16)


def index_body(where, p_ref, index, spare_ref):
    first, root = where[1], where[2]
    p = p_ref[...]
    top = p.shape[1]
    side = 128
    sub = lax.broadcasted_iota(jnp.int32, (side, top), 0)
    lane = lax.broadcasted_iota(jnp.int32, (1, top), 1)

    def column(line, c):
        square = jnp.broadcast_to(line[:, c * side : (c + 1) * side], (side, side)).T
        return jnp.concatenate([square] * (top // side), axis=1)

    def count(hits):
        return jnp.sum(hits, axis=0, keepdims=True)

    chosen = jnp.zeros((1, top), jnp.int32)
    rank = jnp.zeros((1, top), jnp.int32)
    for c in range(top // side):
        pc = column(p, c)
        chosen += count(jnp.where(pc == lane, 1, 0))
        rank += count(jnp.where((pc >= top) & (pc < p), 1, 0))
    free = jnp.where(chosen == 0, 1.0, 0.0)
    before = jnp.zeros((8, top), jnp.float32)
    for c in range(top // side):
        ahead = jnp.where(sub + c * side < lane, 1.0, 0.0).astype(jnp.bfloat16)
        some = jnp.broadcast_to(free[:, c * side : (c + 1) * side], (8, side)).astype(jnp.bfloat16)
        before += jnp.dot(some, ahead, preferred_element_type=jnp.float32)
    place = jnp.where(chosen == 0, before[0:1].astype(jnp.int32), -1)
    spare = jnp.zeros((1, top), jnp.int32)
    for c in range(top // side):
        spare += count(jnp.where(column(place, c) == rank, sub + c * side, 0))
    local = p - first
    owned = (local >= 0) & (local < where[3])
    index[...] = jnp.where(owned, local, jnp.where(root == 1, spare, -1))
    spare_ref[...] = spare


def row_index(where, line):
    shape = jax.ShapeDtypeStruct(line.shape, jnp.int32)
    return pl.pallas_call(
        index_body,
        in_specs=[SMEM, VMEM],
        out_specs=[VMEM] * 2,
        out_shape=[shape] * 2,
        compiler_params=params(6),
        cost_estimate=pl.CostEstimate(flops=6 << 30, bytes_accessed=1 << 20, transcendentals=0),
        name="row_index",
    )(where, line)


def gather_body(h, index, where, matrix, *outs):
    y = where[0]
    for out, d in zip(outs, (2, 1, 3, 0)):
        start = lax.rem(y + d, 4) * 256 + h * 128

        def group(g, carry, out=out, start=start):
            rows = []
            for u in range(8):
                i = index[0, start + g * 8 + u]
                row = matrix[pl.ds(jnp.maximum(i, 0), 1), :]
                rows.append(jnp.where(i >= 0, row, 0.0))
            out[pl.ds(pl.multiple_of(g * 8, 8), 8), :] = jnp.concatenate(rows, axis=0)
            return carry

        lax.fori_loop(0, 16, group, 0)


def gather_rows(h, index, where, matrix):
    n = matrix.shape[1]
    return pl.pallas_call(
        functools.partial(gather_body, h),
        in_specs=[SMEM, SMEM, VMEM],
        out_specs=[VMEM] * 4,
        out_shape=[jax.ShapeDtypeStruct((128, n), jnp.float32)] * 4,
        compiler_params=params(4),
        cost_estimate=pl.CostEstimate(flops=0, bytes_accessed=6 << 20, transcendentals=0),
        name="gather_rows",
    )(index, where, matrix)


def dots(bh, bl, ah, al):
    dot = functools.partial(
        lax.dot_general,
        dimension_numbers=(((0,), (0,)), ((), ())),
        preferred_element_type=jnp.float32,
    )
    return dot(ah, bh) + dot(ah, bl) + dot(al, bh)


def prep_body(order, *refs):
    slices, (bh, bl), full = refs[:8], refs[8:10], refs[10]
    y, da = order[16], order[18]
    for s, d in enumerate((0, da, 4 - da, 2)):
        t = lax.rem(y + d, 4)
        for h in range(2):
            full[pl.ds(pl.multiple_of(t * 256 + h * 128, 128), 128), :] = slices[2 * s + h][...]
    for j in range(16):
        rows = full[pl.ds(pl.multiple_of(order[j] * KP, KP), KP), :]
        bh[j * KP : (j + 1) * KP, :], bl[j * KP : (j + 1) * KP, :] = split(rows)


def prep(order, slices):
    n = slices[0].shape[1]
    return pl.pallas_call(
        prep_body,
        in_specs=[SMEM] + [VMEM] * len(slices),
        out_specs=[VMEM] * 2,
        out_shape=[jax.ShapeDtypeStruct((1024, n), jnp.bfloat16)] * 2,
        scratch_shapes=[pltpu.VMEM((1024, n), jnp.float32)],
        compiler_params=params(8),
        cost_estimate=pl.CostEstimate(flops=0, bytes_accessed=4 << 20, transcendentals=0),
        name="prep",
    )(order, *slices)


def load(first, pieces, into=None):
    m = pieces[0].shape[1]
    n = len(pieces)

    def body(*refs):
        ah, al = refs[-2:]

        def block_step(*io):
            at = pl.ds(pl.multiple_of(pl.program_id(0) * MB, MB), MB)
            for j, piece in enumerate(io, first):
                ah[j * KP : (j + 1) * KP, at], al[j * KP : (j + 1) * KP, at] = split(piece[...])

        if into is not None:
            for j, piece in enumerate(refs[:n], first):
                ah[j * KP : (j + 1) * KP, :], al[j * KP : (j + 1) * KP, :] = split(piece[...])
            return
        spec = pl.BlockSpec((KP, MB), lambda i: (0, i))
        pltpu.emit_pipeline(block_step, grid=(m // MB,), in_specs=[spec] * n)(*refs[:n])

    return pl.pallas_call(
        body,
        in_specs=[HBM] + [ANY] * (n - 1) if into is None else [VMEM] * (n + 2),
        out_specs=[VMEM] * 2,
        out_shape=[jax.ShapeDtypeStruct((16 * KP, m), jnp.bfloat16)] * 2,
        input_output_aliases={} if into is None else {n: 0, n + 1: 1},
        compiler_params=params(6),
        cost_estimate=pl.CostEstimate(flops=(n << 30) if into is None else 0, bytes_accessed=n << 20, transcendentals=0),
    )(*pieces, *([] if into is None else into))


def patch_rows(lo, hi, ref, row, change):
    fours = lax.div(hi - lo, 4)

    def put(ks):
        rows = [pl.ds(row(k), 1) for k in ks]
        values = [ref[r, :] + change(k) for r, k in zip(rows, ks)]
        for r, value in zip(rows, values):
            ref[r, :] = value

    def four(i, carry):
        put([lo + 4 * i + u for u in range(4)])
        return carry

    def one(k, carry):
        put([k])
        return carry

    lax.fori_loop(0, fours, four, 0)
    lax.fori_loop(lo + 4 * fours, hi, one, 0)


def update_left(scalars, panel, bh, bl, matrix):
    rows, n = matrix.shape
    half = rows // 2

    def body(order, starts, keys, spares, ph, pw, bh, bl, matrix, out):
        root = order[17]

        def block_step(block, carry):
            at = pl.ds(pl.multiple_of(block * 2 * MB, 2 * MB), 2 * MB)
            in_top = (root == 1) & (block < 512 // MB)
            acc = dots(bh[...], bl[...], ph[:, at], pw[:, at])
            out[at, :] = jnp.where(in_top, 0.0, matrix[at, :]) + jnp.where(in_top, 1.0, -1.0) * acc
            return carry

        lax.fori_loop(0, half // MB // 2, block_step, 0)

        end = starts[half // MB]

        @pl.when(root == 1)
        def _():
            patch_rows(
                0, end, out, lambda k: keys[k],
                lambda k: matrix[pl.ds(spares[k], 1), :] - matrix[pl.ds(keys[k], 1), :],
            )

        @pl.when(root == 0)
        def _():
            patch_rows(0, end, out, lambda k: keys[k], lambda k: -matrix[pl.ds(keys[k], 1), :])

    return pl.pallas_call(
        body,
        in_specs=[SMEM] * 4 + [VMEM] * 5,
        out_specs=VMEM,
        out_shape=jax.ShapeDtypeStruct((half, n), jnp.float32),
        compiler_params=params(14),
        cost_estimate=pl.CostEstimate(flops=3 * rows * n * 1024, bytes_accessed=1 << 20, transcendentals=0),
        name="update_left",
    )(*scalars, *panel, bh, bl, matrix)


def update_right(scalars, panel, bh, bl, matrix, left, parts):
    rows, n = matrix.shape
    first = rows // 2 // MB

    def body(order, starts, keys, spares, slots, ph, pw, bh, bl, matrix, _, *refs):
        parts, (out, left, disp, sem) = refs[:4], refs[4:]
        root = order[17]
        for i, part in enumerate(parts):
            disp[i * 256 : (i + 1) * 256, :] = part[...]

        @pl.when(root == 0)
        def _():
            patch_rows(0, starts[first], left, lambda k: keys[k], lambda k: disp[pl.ds(slots[k], 1), :])

        away = pltpu.make_async_copy(left, out.at[pl.ds(0, first * MB), :], sem)
        away.start()

        def block_step(dest):
            block = pl.program_id(0) + first
            at = pl.ds(pl.multiple_of(block * MB, MB), MB)
            dest[...] = matrix[at, :] - dots(bh[...], bl[...], ph[:, at], pw[:, at])

            def patch(source, rows_of):
                patch_rows(
                    starts[block], starts[block + 1], dest, lambda k: keys[k] - block * MB,
                    lambda k: source[pl.ds(rows_of[k], 1), :] - matrix[pl.ds(keys[k], 1), :],
                )

            @pl.when(root == 1)
            def _():
                patch(matrix, spares)

            @pl.when(root == 0)
            def _():
                patch(disp, slots)

        pltpu.emit_pipeline(
            block_step, grid=(first,), in_specs=[], out_specs=[pl.BlockSpec((MB, n), lambda i: (i + first, 0))]
        )(out)
        away.wait()

    return pl.pallas_call(
        body,
        in_specs=[SMEM] * 5 + [VMEM] * 10,
        out_specs=[ANY, VMEM],
        out_shape=[jax.ShapeDtypeStruct(matrix.shape, jnp.float32), jax.ShapeDtypeStruct(left.shape, jnp.float32)],
        scratch_shapes=[pltpu.VMEM((1024, n), jnp.float32), pltpu.SemaphoreType.DMA],
        input_output_aliases={10: 1},
        compiler_params=params(14),
        cost_estimate=pl.CostEstimate(flops=3 * rows * n * 1024, bytes_accessed=8 << 20, transcendentals=0),
        name="update_right",
    )(*scalars, *panel, bh, bl, matrix, left, *parts)[0]


def step(matrix, pivots, lower_panel):
    top = pivots.shape[0]
    local_rows, _ = matrix.shape
    row, col = lax.axis_index("row"), lax.axis_index("col")
    x_hi, y = row // 4, row % 4
    x_lo, z, core = col // 8, (col // 2) % 4, col % 2
    first_row = row * local_rows
    root = row == 0
    quarter, eighth = top // 4, top // 8

    own = lower_panel
    xs = send(own, x_lo_swap)
    za = send(own, z_way)
    zb = send(own, z_back)
    xa = send(xs, z_way)
    xb = send(xs, z_back)
    z2 = send(za, z_way)
    x2 = send(xa, z_way)
    pieces = []
    for piece in (own, xs, za, zb, xa, xb, z2, x2):
        pieces += [piece, send(piece, core_swap)]

    where = jnp.stack([y, first_row, root.astype(jnp.int32), jnp.int32(local_rows)]).astype(jnp.int32)
    index, spare = row_index(where, pivots.reshape(1, top))

    got_a = gather_rows(0, index, where, matrix)
    got_b = gather_rows(1, index, where, matrix)

    def exchange(h, got):
        root_owned = (lax.dynamic_slice(pivots, (y * quarter + h * eighth,), (eighth,)) < local_rows)[:, None]
        m2 = send_row(got[0], 0, 2)
        m1 = send_row(got[1], 0, 1)
        m3 = send_row(got[2], 0, -1)
        pivot_sum, disp = 0.0, 0.0
        for message, source in ((got[3], y), (m1, (y + 3) % 4), (m2, (y + 2) % 4), (m3, (y + 1) % 4)):
            from_root = (x_hi == 0) & (source == 0)
            is_disp = from_root & ~root_owned
            pivot_sum = pivot_sum + jnp.where(is_disp, 0.0, message)
            disp = disp + jnp.where(is_disp, message, 0.0)
        return pivot_sum, disp

    part_a, disp_a = exchange(0, got_a)
    part_b, disp_b = exchange(1, got_b)
    disp = jnp.concatenate([disp_a, disp_b], axis=0)
    full_a = part_a + send(part_a, x_hi_swap)
    full_b = part_b + send(part_b, x_hi_swap)
    cross = send_row(disp, 1, 0, lambda x: x == 0)
    disp = jnp.where(x_hi == 0, disp, cross)
    a_a, b_a = send(full_a, y_way), send(full_a, y_back)
    a_b, b_b = send(full_b, y_way), send(full_b, y_back)
    f_a, f_b = send(a_a, y_way), send(a_b, y_way)
    a_d, b_d = send(disp, y_way), send(disp, y_back)
    f_d = send(a_d, y_way)
    a_off = jnp.where(core == 0, 3, 1)

    dz = jnp.where(core == 0, -1, 1)

    def block(dx, dzs, dc):
        return ((x_lo + dx) % 2) * 8 + ((z + dzs + 4) % 4) * 2 + (core + dc) % 2

    order = []
    for dx, sign in ((0, 0), (1, 0), (0, 1), (0, -1), (1, 1), (1, -1), (0, 2), (1, 2)):
        order += [block(dx, sign * dz, 0), block(dx, -sign * dz, 1)]
    order = jnp.stack(order + [y, root.astype(jnp.int32), a_off]).astype(jnp.int32)

    owned = (pivots >= first_row) & (pivots < first_row + local_rows)
    key = jnp.where(owned & (pivots >= top), pivots - first_row, jnp.int32(2**30))
    slot = jnp.arange(top, dtype=jnp.int32)
    off = (slot // quarter - y + 4) % 4
    part = jnp.where(off == 0, 0, jnp.where(off == 2, 3, jnp.where(off == a_off, 1, 2)))
    keys, slots, spares = lax.sort((key, part * quarter + slot % quarter, spare.reshape(top)), num_keys=1)
    edges = jnp.arange(local_rows // MB + 1, dtype=jnp.int32) * MB
    starts = jnp.sum((key[None, :] < edges[:, None]).astype(jnp.int32), axis=1)

    bh, bl = prep(order, [full_a, full_b, a_a, a_b, b_a, b_b, f_a, f_b])
    panel = load(0, pieces[:10])
    panel = load(10, pieces[10:14], panel)
    panel = load(14, pieces[14:], panel)
    left = update_left((order, starts, keys, spares), panel, bh, bl, matrix)
    return update_right((order, starts, keys, spares, slots), panel, bh, bl, matrix, left, [disp, a_d, b_d, f_d])


def solution(mesh):
    in_specs = (P("row", "col"), P(), P("col", "row"))
    out_specs = P("row", "col")
    return jax.shard_map(step, mesh=mesh, in_specs=in_specs, out_specs=out_specs, check_vma=False)
```
